32 devices in a mesh: node: 4 (over x, core), dev: 8 (over z, y).
Axes of the slice: x: 2, y: 2, z: 4, core: 2. Of those that a mesh axis runs over, the one named last changes fastest.
Arguments:
- expert_hidden: bfloat16 [32768, 1536], P(('node', 'dev')), may hold values from -6 to 6
- expert_down: bfloat16 [32, 1536, 5120], P(('node', 'dev')), may hold values from -0.15625 to 0.15625
- shared_hidden: bfloat16 [4096, 1536], P(('node', 'dev')), may hold values from -6 to 6
- shared_down: bfloat16 [1536, 5120], P('dev'), may hold values from -0.15625 to 0.15625
- expert_ids: int32 [4096, 6], P(('node', 'dev')), may hold values from 0 to 31, as said below
- gates: float32 [4096, 6], P(('node', 'dev')), may hold values from 0.1 to 2
Outputs:
- combined: bfloat16 [4096, 5120], P(('node', 'dev'))
The draws below stay inside these ranges and needn't reach their ends.
Inputs may be any that keep to these rules, and one draw needn't show every extreme that they name: `expert_ids`: each row names 6 different experts, two in each of three different groups, expert e lying in group e // 8. Among the 128 rows of one device every group is named by exactly 96 rows and no expert by more than 32 rows; some expert is named by exactly 32 rows of every device.
All inputs are finite; a program needn't handle non-finite values.
Results may differ from the reference program's by a relative error of at most 0.0047.
Values may be sent and summed in bfloat16 or wider, within the bound.
No kernel may reach another device: no remote copies, remote signals or barrier semaphores. Data moves between devices by JAX's collectives and lax.ppermute only.
A program may use at most 128 MiB of HBM per device.

```python
import math
import jax
import jax.numpy as jnp
from jax import lax

D = 5120
EF = 1536
SH = 1536
TOP = 6
TOK_DEV = 128
NODES = 4
NODE_EXP = 8
EXPERTS = 32
CAP = 32
SLOTS = 1024
TOKENS = 4096


def one_block(block_key, full_expert):
    order_key, score_key, shift_key, token_key, column_key = jax.random.split(block_key, 5)
    half_cap = CAP // 2
    label_count = NODE_EXP * half_cap
    node_share = 3 * TOK_DEV // NODES
    node_order = jax.random.permutation(order_key, NODES).astype(jnp.int32)
    scores = jax.random.randint(score_key, (NODES, label_count), 0, 65536)
    label_expert = jnp.arange(label_count, dtype=jnp.int32) % NODE_EXP
    shifts = jax.random.randint(shift_key, (NODES,), 1, NODE_EXP)
    full_node = full_expert // NODE_EXP
    full_local = full_expert % NODE_EXP
    partner = (full_local - shifts) % NODE_EXP
    forced = (node_order[:, None] == full_node) & ((label_expert[None, :] == full_local) | (label_expert[None, :] == partner[:, None]))
    ranked = (scores - forced.astype(jnp.int32) * 131072) * label_count + jnp.arange(label_count, dtype=jnp.int32)[None, :]
    sequence = jnp.argsort(ranked, axis=1)
    first_expert = (sequence % NODE_EXP)[:, :node_share]
    second_expert = (first_expert + shifts[:, None]) % NODE_EXP
    places = jnp.arange(TOK_DEV, dtype=jnp.int32)[:, None] * 3 + jnp.arange(3, dtype=jnp.int32)[None, :]
    node_place = places % NODES
    node_rank = places // NODES
    chosen_node = node_order[node_place]
    first_pick = chosen_node * NODE_EXP + first_expert[node_place, node_rank]
    second_pick = chosen_node * NODE_EXP + second_expert[node_place, node_rank]
    picked = jnp.stack([first_pick, second_pick], axis=2).reshape(TOK_DEV, TOP)
    picked = picked[jax.random.permutation(token_key, TOK_DEV)]
    column_scores = jax.random.randint(column_key, (TOK_DEV, TOP), 0, 65536) * TOP + jnp.arange(TOP, dtype=jnp.int32)[None, :]
    column_order = jnp.argsort(column_scores, axis=1)
    return jnp.take_along_axis(picked, column_order, axis=1).astype(jnp.int32)


def draw_expert_ids(key, part):
    full_expert = jax.random.randint(jax.random.fold_in(key, 7), (), 0, EXPERTS)
    block_keys = jax.random.split(jax.random.fold_in(key, 11), TOKENS // TOK_DEV)
    picked = jax.vmap(lambda block_key: one_block(block_key, full_expert))(block_keys)
    return picked.reshape(TOKENS, TOP)


def level_of(rng, shape, pieces, smallest, largest):
    def one(dim, parts):
        draws = jax.random.uniform(jax.random.fold_in(jax.random.fold_in(rng, 6), dim), (parts,), jnp.float32, smallest / len(pieces), largest / len(pieces))
        return jnp.repeat(jnp.exp(draws), shape[dim] // parts).reshape((-1,) + (1,) * (len(shape) - dim - 1))

    factor_of = one(*pieces[0])
    for cut in pieces[1:]:
        factor_of = factor_of * one(*cut)
    return factor_of


def normal_values(own_key, shape, width, reach, pieces=(), held_as=jnp.bfloat16):
    result = jax.random.normal(own_key, shape, jnp.float32) * width
    if len(pieces) > 0:
        result = level_of(own_key, shape, pieces, -0.22, 0.18) * result
    return jnp.clip(result, min=-reach, max=reach).astype(held_as)


def setup_inputs(seed: int = 0) -> dict:
    key_list = jax.random.split(jax.random.key(seed), 7)
    return {
        "expert_hidden": normal_values(key_list[0], (EXPERTS * SLOTS, EF), 1.0, 6.0, ((0, 32),)),
        "expert_down": normal_values(key_list[1], (EXPERTS, EF, D), EF ** -0.5, 0.15625, ((0, 32),)),
        "shared_hidden": normal_values(key_list[2], (TOKENS, SH), 1.0, 6.0, ((0, 32),)),
        "shared_down": normal_values(key_list[3], (SH, D), SH ** -0.5, 0.15625, ((0, 8),)),
        "expert_ids": draw_expert_ids(jax.random.fold_in(key_list[6], 71), 0),
        "gates": jnp.clip(jnp.exp(math.log(2.0) - 2.9957323 * jax.random.uniform(key_list[5], (TOKENS, TOP), jnp.float32) ** level_of(key_list[5], (TOKENS, TOP), ((0, 32),), -0.2, 0.2)), 0.1, 2.0),
    }


def reference(expert_hidden, expert_down, shared_hidden, shared_down, expert_ids, gates):
    blocks = expert_ids.reshape(EXPERTS, TOK_DEV, TOP)
    labels = jnp.arange(EXPERTS, dtype=jnp.int32)
    chosen = (blocks[..., None] == labels).astype(jnp.int32)
    counts = jnp.sum(chosen, axis=2)
    before = jnp.cumsum(counts, axis=1) - counts
    position = jnp.sum(chosen * before[:, :, None, :], axis=3).astype(jnp.int32)
    source = jnp.arange(EXPERTS, dtype=jnp.int32)[:, None, None]
    slot_index = (blocks * SLOTS + source * CAP + position).reshape(-1).astype(jnp.int32)
    owner_rows = jnp.repeat(jnp.arange(TOKENS, dtype=jnp.int32), TOP)
    slot_owner = jnp.zeros((EXPERTS * SLOTS,), jnp.int32).at[slot_index].set(owner_rows)
    slot_gate = jnp.zeros((EXPERTS * SLOTS,), jnp.float32).at[slot_index].set(gates.reshape(-1).astype(jnp.float32))
    hidden_blocks = expert_hidden.reshape(EXPERTS, SLOTS, EF)

    def one_expert(running, inputs):
        hidden, weight, owners, weights = inputs
        product = jnp.dot(hidden.astype(jnp.float32), weight.astype(jnp.float32), preferred_element_type=jnp.float32)
        rounded = lax.optimization_barrier(product.astype(jnp.bfloat16)).astype(jnp.float32)
        return running.at[owners].add(weights[:, None] * rounded), None

    routed, unused = lax.scan(one_expert, jnp.zeros((TOKENS, D), jnp.float32),
                              (hidden_blocks, expert_down, slot_owner.reshape(EXPERTS, SLOTS), slot_gate.reshape(EXPERTS, SLOTS)))
    shared = jnp.dot(shared_hidden, shared_down, preferred_element_type=jnp.float32)
    return (shared + routed).astype(jnp.bfloat16)
```

```python
import functools

import jax
import jax.numpy as jnp
from jax import lax
from jax.experimental import pallas as pl
from jax.experimental.pallas import tpu as pltpu
from jax.sharding import PartitionSpec as P

CHUNKS = 10
LANES = 128


def reversed_bits(value, count):
    result = 0
    for bit in range(count):
        result |= ((value >> bit) & 1) << (count - 1 - bit)
    return result


def expert_kernel(pieces, order_ref, hidden_ref, down_ref, *out_refs):
    rows = hidden_ref.shape[0] // (pieces * len(out_refs))
    for k, out_ref in enumerate(out_refs):
        parts = []
        for q in range(pieces):
            first = pl.multiple_of(order_ref[k * pieces + q] * rows, rows)
            parts.append(hidden_ref[pl.ds(first, rows), :])
        left = jnp.concatenate(parts, axis=0)
        out_ref[...] = jnp.dot(
            left, down_ref[...], preferred_element_type=jnp.float32
        ).astype(out_ref.dtype)


def expert_chunk(order, hidden, down, start, width, tile, nodes, members):
    rows, depth = hidden.shape
    share = rows // nodes
    first = start // tile
    return pl.pallas_call(
        functools.partial(expert_kernel, members),
        out_shape=[jax.ShapeDtypeStruct((share, width), jnp.bfloat16)] * nodes,
        grid_spec=pltpu.PrefetchScalarGridSpec(
            num_scalar_prefetch=1,
            grid=(width // tile,),
            in_specs=[
                pl.BlockSpec((rows, depth), lambda j, order_ref: (0, 0)),
                pl.BlockSpec((depth, tile), lambda j, order_ref: (0, first + j)),
            ],
            out_specs=[pl.BlockSpec((share, tile), lambda j, order_ref: (0, j))] * nodes,
        ),
        cost_estimate=pl.CostEstimate(
            flops=2 * rows * depth * width,
            bytes_accessed=2 * (rows * depth + depth * width + rows * width),
            transcendentals=0,
        ),
        name="expert",
    )(order, hidden, down)


def gate_kernel(nodes, members, capacity, depth, choices, place_ref, seen_ref, left_ref):
    bits = members.bit_length() - 1
    node, dev = place_ref[0], place_ref[1]
    tokens = seen_ref.shape[1]
    slots = nodes * capacity
    row = lax.broadcasted_iota(jnp.int32, (tokens, tokens), 0)
    column = lax.broadcasted_iota(jnp.int32, (tokens, tokens), 1)
    earlier = (row > column).astype(jnp.float32)
    lane = lax.broadcasted_iota(jnp.int32, (tokens, slots), 1)
    for q in range(members):
        block = seen_ref[dev ^ reversed_bits(q, bits)].astype(jnp.float32)
        ids = block[:, depth : depth + choices]
        high = block[:, depth + choices : depth + 2 * choices]
        low = block[:, depth + 2 * choices : depth + 3 * choices]
        spread = jnp.zeros((tokens, slots), jnp.float32)
        upper, lower = [], []
        for k in range(nodes):
            label = ((node ^ k) * members + dev).astype(jnp.float32)
            match = (ids == label).astype(jnp.float32)
            chosen = jnp.sum(match, axis=1, keepdims=True)
            upper.append(jnp.sum(match * high, axis=1, keepdims=True))
            lower.append(jnp.sum(match * low, axis=1, keepdims=True))
            spread = jnp.where(lane // capacity == k, chosen, spread)
        before = jnp.dot(earlier, spread, preferred_element_type=jnp.float32)
        here = (spread > 0.5) & (before == (lane % capacity).astype(jnp.float32))
        top = jnp.zeros((tokens, slots), jnp.float32)
        rest = jnp.zeros((tokens, slots), jnp.float32)
        for k in range(nodes):
            mine = here & (lane // capacity == k)
            top = jnp.where(mine, upper[k], top)
            rest = jnp.where(mine, lower[k], rest)
        rows = slice(q * tokens, (q + 1) * tokens)
        left_ref[rows, 0:slots] = top.astype(jnp.bfloat16)
        left_ref[rows, slots : 2 * slots] = rest.astype(jnp.bfloat16)
        left_ref[rows, 2 * slots : 2 * slots + depth] = seen_ref[
            dev ^ reversed_bits(q, bits)
        ][:, 0:depth]


def gate_matrix(place, seen, nodes, members, capacity, depth, choices):
    tokens = seen.shape[1]
    return pl.pallas_call(
        functools.partial(gate_kernel, nodes, members, capacity, depth, choices),
        out_shape=jax.ShapeDtypeStruct(
            (members * tokens, 2 * nodes * capacity + depth), jnp.bfloat16
        ),
        in_specs=[
            pl.BlockSpec(memory_space=pltpu.SMEM),
            pl.BlockSpec(memory_space=pltpu.VMEM),
        ],
        out_specs=pl.BlockSpec(memory_space=pltpu.VMEM),
        name="gate",
    )(place, seen)


def merge_kernel(members, nodes, left_ref, down_ref, *refs):
    arrived, outs = refs[:nodes], refs[nodes:]
    tokens = left_ref.shape[0] // members
    rows = arrived[0].shape[0] // members
    targets = []
    for out_ref in outs:
        for first in range(0, out_ref.shape[0], tokens):
            targets.append((out_ref, first))
    for q, (out_ref, first) in enumerate(targets):
        slots = [ref[q * rows : (q + 1) * rows, :] for ref in arrived]
        right = jnp.concatenate(slots + slots + [down_ref[...]], axis=0)
        total = jnp.dot(
            left_ref[q * tokens : (q + 1) * tokens, :],
            right,
            preferred_element_type=jnp.float32,
        )
        out_ref[first : first + tokens, :] = total.astype(out_ref.dtype)


def merge_chunk(left, shared_down, arrived, start, width, tile, members):
    nodes = len(arrived)
    tall, wide = left.shape
    tokens = tall // members
    depth = shared_down.shape[0]
    first = start // tile
    sizes = [1]
    while sum(sizes) < members:
        sizes.append(sum(sizes))
    outs = [jax.ShapeDtypeStruct((tokens * size, width), jnp.bfloat16) for size in sizes]
    share = arrived[0].shape[0]
    return pl.pallas_call(
        functools.partial(merge_kernel, members, nodes),
        out_shape=outs,
        grid=(width // tile,),
        in_specs=[
            pl.BlockSpec((tall, wide), lambda j: (0, 0)),
            pl.BlockSpec((depth, tile), lambda j: (0, first + j)),
        ]
        + [pl.BlockSpec((share, tile), lambda j: (0, j))] * nodes,
        out_specs=[pl.BlockSpec((out.shape[0], tile), lambda j: (0, j)) for out in outs],
        cost_estimate=pl.CostEstimate(
            flops=2 * tall * wide * width,
            bytes_accessed=2 * (tall * wide + depth * width + nodes * share * width + tall * width),
            transcendentals=0,
        ),
        name="merge",
    )(left, shared_down, *arrived)


def body(expert_hidden, expert_down, shared_hidden, shared_down, expert_ids, gates):
    nodes = lax.axis_size("node")
    members = lax.axis_size("dev")
    bits = members.bit_length() - 1
    node, dev = lax.axis_index("node"), lax.axis_index("dev")
    capacity = expert_hidden.shape[0] // (nodes * members)
    tokens, choices = expert_ids.shape
    depth = shared_down.shape[0]
    model_width = expert_down.shape[2]

    def swapped(value, axis, size, mask):
        return lax.ppermute(value, axis, [(i, i ^ mask) for i in range(size)])

    place = jnp.stack([node, dev]).astype(jnp.int32)
    order = jnp.stack(
        [
            (node ^ k) * members + (dev ^ reversed_bits(q, bits))
            for k in range(nodes)
            for q in range(members)
        ]
    ).astype(jnp.int32)

    high = gates.astype(jnp.bfloat16)
    low = (gates - high.astype(jnp.float32)).astype(jnp.bfloat16)
    notes = jnp.concatenate([expert_ids.astype(jnp.bfloat16), high, low], axis=1)
    span = -(-(depth + 3 * choices) // LANES) * LANES
    notes = jnp.pad(notes, ((0, 0), (0, span - depth - 3 * choices)))
    pieces = shared_hidden.reshape(tokens, members, depth).transpose(1, 0, 2)
    sent = jnp.concatenate(
        [pieces, jnp.broadcast_to(notes[None], (members,) + notes.shape)], axis=2
    )
    seen = lax.all_to_all(sent, "dev", split_axis=0, concat_axis=0, tiled=True)
    left = gate_matrix(place, seen, nodes, members, capacity, depth, choices)

    tile = 256
    units = model_width // tile
    count = min(CHUNKS, units)
    edges = [tile * (units * c // count) for c in range(count + 1)]
    results = []
    for c in range(count):
        start, width = edges[c], edges[c + 1] - edges[c]
        outputs = expert_chunk(
            order, expert_hidden, expert_down[0], start, width, tile, nodes, members
        )
        arrived = [outputs[0]] + [
            swapped(outputs[k], "node", nodes, k) for k in range(1, nodes)
        ]
        parts = merge_chunk(left, shared_down, arrived, start, width, tile, members)
        for bit in range(bits):
            moved = swapped(parts[-1], "dev", members, 1 << bit).astype(jnp.float32)
            kept, base = [], 0
            for part in parts[:-1]:
                piece = moved[base : base + part.shape[0]]
                kept.append((part.astype(jnp.float32) + piece).astype(jnp.bfloat16))
                base += part.shape[0]
            parts = kept
        results.append(parts[0])
    return jnp.concatenate(results, axis=1)


def solution(mesh):
    in_specs = (
        P(("node", "dev"), None),
        P(("node", "dev"), None, None),
        P(("node", "dev"), None),
        P("dev", None),
        P(("node", "dev"), None),
        P(("node", "dev"), None),
    )
    out_specs = P(("node", "dev"), None)
    return jax.shard_map(body, mesh=mesh, in_specs=in_specs, out_specs=out_specs, check_vma=False)
```
